32 devices in a mesh: pair: 4 (over x, core), box: 8 (over z, y).
Axes of the slice: x: 2, y: 2, z: 4, core: 2. Of those that a mesh axis runs over, the one named last changes fastest.
Arguments:
- sources: bfloat16 [3072, 64, 256], P(('pair', 'box')), may hold values from -6 to 6
- basis_in: bfloat16 [3072, 4096], P(('pair', 'box')), may hold values from -0.75 to 0.75
- kinds: int32 [5, 3072], P(None, ('pair', 'box')), may hold values from 0 to 7
- couplings: bfloat16 [5, 8, 64, 128], replicated, may hold values from -0.5 to 0.5
- basis_out: bfloat16 [3072, 4096], P(('pair', 'box')), may hold values from -0.75 to 0.75
Outputs:
- wavefield: bfloat16 [3072, 64, 256], P(('pair', 'box'))
The draws below stay inside these ranges and needn't reach their ends.
Inputs may be any that keep to these rules, and one draw needn't show every extreme that they name: Row l of kinds is indexed by source node for l < 2 and by target position for later levels.
All inputs are finite; a program needn't handle non-finite values.
Results may differ from the reference program's by a relative error of at most 0.015.
Values may be sent and summed in bfloat16 or wider, within the bound.
A program may use at most 192 MiB of HBM per device.

```python
import jax
import jax.numpy as jnp
from jax import lax

R = 64
PTS = 64
SHOTS = 256
KINDS = 8
BOX_DEV = 96
PAIR_SPAN = 4
BOX_SPAN = 8
PAIR_LEVELS = 2
BOX_LEVELS = 3
LEVELS = 5
GROUP = 12
BOXES = 3072


def plant(drawn, stream_key, smallest, largest):
    longest = drawn.shape.index(max(drawn.shape))
    spots = []
    for shift in (0, 1):
        where = [jax.random.randint(jax.random.fold_in(stream_key, axis), (), 0, length) for axis, length in enumerate(drawn.shape)]
        where[longest] = (where[longest] + shift) % drawn.shape[longest]
        spots.append(tuple(where))
    return drawn.at[spots[0]].set(smallest).at[spots[1]].set(largest)


def steps_of(key, shape, split, least, largest):
    def one(dim, shards_of):
        steps = jax.random.uniform(jax.random.fold_in(jax.random.fold_in(key, 6), dim), (shards_of,), jnp.float32, least / len(split), largest / len(split))
        return jnp.repeat(jnp.exp(steps), shape[dim] // shards_of).reshape((-1,) + (1,) * (len(shape) - dim - 1))

    gain = one(*split[0])
    for cut in split[1:]:
        gain = gain * one(*cut)
    return gain


def bell_draw(own_key, shape, deviation, limit, shards=(), kind=jnp.bfloat16):
    array = jax.random.normal(own_key, shape, jnp.float32) * deviation
    if len(shards) > 0:
        array = steps_of(own_key, shape, shards, -0.22, 0.18) * array
    return jnp.clip(array, min=-limit, max=limit).astype(kind)


def setup_inputs(seed: int = 0) -> dict:
    key_list = jax.random.split(jax.random.key(seed), 6)
    sources = bell_draw(key_list[0], (BOXES, PTS, SHOTS), 1.0, 6.0, ((0, 32),))
    basis_in = bell_draw(key_list[1], (BOXES, PTS * R), PTS ** -0.5, 0.75, ((0, 32),))
    kinds = plant(jax.random.randint(key_list[2], (LEVELS, BOXES), 0, KINDS), jax.random.fold_in(key_list[2], 1), 0, KINDS - 1).astype(jnp.int32)
    couplings = bell_draw(key_list[3], (LEVELS, KINDS, R, 2 * R), (2 * R) ** -0.5, 0.5)
    basis_out = bell_draw(key_list[4], (BOXES, PTS * R), R ** -0.5, 0.75, ((0, 32),))
    return dict(sources=sources, basis_in=basis_in, kinds=kinds, couplings=couplings, basis_out=basis_out)


def butterfly_level(coeffs, weights, stride):
    leading = coeffs.shape[0]
    groups = leading // (2 * stride)
    shaped = coeffs.reshape((groups, 2, stride) + coeffs.shape[1:])
    stacked = jnp.concatenate([shaped[:, 0], shaped[:, 1]], axis=-2)
    paired = weights.reshape((groups, 2, stride) + weights.shape[1:])
    product = jnp.einsum("htlkij,hlkjs->htlkis", paired.astype(jnp.float32), stacked.astype(jnp.float32))
    return product.astype(jnp.bfloat16).reshape(coeffs.shape)


def reference(sources, basis_in, kinds, couplings, basis_out):
    source_grid = sources.reshape(PAIR_SPAN, BOX_SPAN, BOX_DEV, PTS, SHOTS)
    basis_grid = basis_in.reshape(PAIR_SPAN, BOX_SPAN, BOX_DEV, PTS, R)

    def source_section(box_index):
        shot_block = lax.dynamic_index_in_dim(source_grid, box_index, 1, keepdims=False)
        basis_block = lax.dynamic_index_in_dim(basis_grid, box_index, 1, keepdims=False)
        coeffs = jnp.einsum("akpr,akps->akrs", basis_block.astype(jnp.float32), shot_block.astype(jnp.float32)).astype(jnp.bfloat16)
        for level_row in range(PAIR_LEVELS):
            kind_grid = kinds[level_row].reshape(PAIR_SPAN, BOX_SPAN, BOX_DEV)
            kind_rows = lax.dynamic_index_in_dim(kind_grid, box_index, 1, keepdims=False)
            coeffs = butterfly_level(coeffs, couplings[level_row][kind_rows], 2 ** level_row)
        return coeffs

    middle = lax.map(source_section, jnp.arange(BOX_SPAN, dtype=jnp.int32))

    def target_section(pair_index):
        coeffs = lax.dynamic_index_in_dim(middle, pair_index, 1, keepdims=False)
        for depth_bit in range(BOX_LEVELS):
            level_row = PAIR_LEVELS + depth_bit
            kind_grid = kinds[level_row].reshape(PAIR_SPAN, BOX_SPAN, BOX_SPAN, GROUP)
            kind_block = lax.dynamic_index_in_dim(kind_grid, pair_index, 0, keepdims=False)
            kind_rows = jnp.transpose(kind_block, (1, 0, 2)).reshape(BOX_SPAN, BOX_DEV)
            coeffs = butterfly_level(coeffs, couplings[level_row][kind_rows], 2 ** depth_bit)
        ordered = coeffs.reshape(BOX_SPAN, BOX_SPAN, GROUP, R, SHOTS)
        ordered = jnp.transpose(ordered, (1, 0, 2, 3, 4)).reshape(BOX_SPAN * BOX_DEV, R, SHOTS)
        out_grid = basis_out.reshape(PAIR_SPAN, BOX_SPAN * BOX_DEV, PTS, R)
        out_basis = lax.dynamic_index_in_dim(out_grid, pair_index, 0, keepdims=False)
        field = jnp.einsum("tpr,trs->tps", out_basis.astype(jnp.float32), ordered.astype(jnp.float32))
        return field.astype(jnp.bfloat16)

    result = lax.map(target_section, jnp.arange(PAIR_SPAN, dtype=jnp.int32))
    return result.reshape(BOXES, PTS, SHOTS)
```

```python
import functools

import jax
import jax.numpy as jnp
from jax import lax
from jax.experimental import pallas as pl
from jax.experimental.pallas import tpu as pltpu
from jax.sharding import PartitionSpec as P

MESH = pl.DeviceIdType.MESH


def dot(left, right):
    return jnp.dot(left, right, preferred_element_type=jnp.float32).astype(jnp.bfloat16)


def for_nodes(count, step, run):
    step = min(step, count)
    if step == count:
        for node in range(count):
            run(node)
        return

    def several(outer, carry):
        for inner in range(step):
            run(outer * step + inner)
        return carry

    lax.fori_loop(0, count // step, several, 0)


def kernel(
    pair_size, box_size, rank,
    sources, basis_in, kinds, couplings, basis_out, wavefield,
    shots_in, bases_in, bases_out, last, moved, work, field,
    *rest,
):
    pair_levels = pair_size.bit_length() - 1
    box_levels = box_size.bit_length() - 1
    stacks = rest[:pair_levels]
    in_sem, vin_sem, uin_sem, out_sem, pair_send, pair_recv, box_send, box_recv = rest[pair_levels:]
    pair = lax.axis_index("pair")
    box = lax.axis_index("box")
    chunks = shots_in.shape[0]

    def load_shots(j):
        return pltpu.make_async_copy(sources.at[:, j], shots_in.at[j], in_sem.at[j])

    def load_in(j):
        return pltpu.make_async_copy(basis_in.at[:, j], bases_in.at[j], vin_sem.at[j])

    def load_out(j):
        return pltpu.make_async_copy(basis_out.at[:, j], bases_out.at[j], uin_sem.at[j])

    def store(j):
        return pltpu.make_async_copy(field.at[j], wavefield.at[:, j], out_sem.at[j])

    def half(level):
        bit = lax.rem(pair // 2**level, 2)
        return bit, pl.ds(pl.multiple_of(bit * rank, rank), rank)

    def partner(level):
        bit, _ = half(level)
        return pair + 2**level * (1 - 2 * bit)

    def exchange(level, j):
        _, rows = half(level)
        return pltpu.make_async_remote_copy(
            src_ref=stacks[level].at[j, :, rows],
            dst_ref=stacks[level].at[j, :, rows],
            send_sem=pair_send.at[level, j],
            recv_sem=pair_recv.at[level, j],
            device_id=(partner(level), box),
            device_id_type=MESH,
        )

    def peer(step):
        return lax.rem(box + step, box_size)

    def scatter(j, step):
        return pltpu.make_async_remote_copy(
            src_ref=last.at[j, peer(step)],
            dst_ref=moved.at[j, box],
            send_sem=box_send.at[j, step],
            recv_sem=box_recv.at[j, step],
            device_id=(pair, peer(step)),
            device_id_type=MESH,
        )

    def each_peer(run):
        def one(step, carry):
            run(step)
            return carry

        lax.fori_loop(1, box_size, one, 0)

    def first(j):
        load_shots(j).wait()
        load_in(j).wait()
        _, rows = half(0)

        def node(g):
            product = lax.dot_general(
                bases_in[j, g], shots_in[j, g], (((0,), (0,)), ((), ())),
                preferred_element_type=jnp.float32,
            )
            stacks[0][j, g, rows] = product.astype(jnp.bfloat16)

        for_nodes(box_size, 8, node)
        exchange(0, j).start()

    def pair_level(level, j):
        exchange(level, j).wait_recv()
        final = level == pair_levels - 1
        if not final:
            _, rows = half(level + 1)

        def node(g):
            weights = couplings[level, kinds[level, g * chunks + j]]
            value = dot(weights, stacks[level][j, g])
            if final:
                last[j, g] = value
            else:
                stacks[level + 1][j, g, rows] = value

        for_nodes(box_size, 8, node)
        if final:
            each_peer(lambda step: scatter(j, step).start())
            moved[j, box] = last[j, box]
        else:
            exchange(level + 1, j).start()

    def box_stage(j):
        load_out(j).wait()
        each_peer(lambda step: scatter(j, step).wait_recv())
        for depth in range(box_levels):
            stride = 2**depth
            row = pair_levels + depth

            def pair_of(index):
                low = index // stride * (2 * stride) + index % stride
                high = low + stride
                if depth == 0:
                    one, two = moved[j, low], moved[j, high]
                else:
                    one, two = work[depth - 1, low], work[depth - 1, high]
                stack = jnp.concatenate([one, two], axis=0)
                weights = jnp.concatenate(
                    [
                        couplings[row, kinds[row, low * chunks + j]],
                        couplings[row, kinds[row, high * chunks + j]],
                    ],
                    axis=0,
                )
                value = dot(weights, stack)
                work[depth, low] = value[:rank]
                work[depth, high] = value[rank:]

            for_nodes(box_size // 2, 4, pair_of)

        def node(b):
            field[j, b] = dot(bases_out[j, b], work[box_levels - 1, b])

        for_nodes(box_size, 8, node)
        store(j).start()

    def each_chunk(run):
        def one(j, carry):
            run(j)
            return carry

        lax.fori_loop(0, chunks, one, 0)

    def load(j):
        load_shots(j).start()
        load_in(j).start()

    each_chunk(load)
    each_chunk(lambda j: load_out(j).start())

    barrier = pltpu.get_barrier_semaphore()
    for level in range(pair_levels):
        pl.semaphore_signal(barrier, inc=1, device_id=(partner(level), box), device_id_type=MESH)

    def greet(step):
        pl.semaphore_signal(barrier, inc=1, device_id=(pair, peer(step)), device_id_type=MESH)

    each_peer(greet)
    pl.semaphore_wait(barrier, pair_levels + box_size - 1)

    starts = [0, 1]
    for level in range(1, pair_levels):
        starts.append(starts[-1] + 2)
    starts.append(starts[-1] + 2)

    def iteration(i, carry):
        def at(start, run):
            j = i - start

            @pl.when(jnp.logical_and(j >= 0, j < chunks))
            def _():
                run(j)

        at(starts[0], first)
        for level in range(pair_levels):
            at(starts[1 + level], functools.partial(pair_level, level))
        at(starts[-1], box_stage)
        return carry

    lax.fori_loop(0, chunks + starts[-1], iteration, 0)

    def finish(j):
        store(j).wait()
        for level in range(pair_levels):
            exchange(level, j).wait_send()
        each_peer(lambda step: scatter(j, step).wait_send())

    each_chunk(finish)


def body(sources, basis_in, kinds, couplings, basis_out):
    pair_size = lax.axis_size("pair")
    box_size = lax.axis_size("box")
    box_count, points, shots = sources.shape
    rank = couplings.shape[2]
    pair_levels = pair_size.bit_length() - 1
    box_levels = box_size.bit_length() - 1
    chunks = box_count // box_size
    dtype = jnp.bfloat16
    block = (chunks, box_size, rank, shots)
    any_space = pl.BlockSpec(memory_space=pl.ANY)
    wavefield = pl.pallas_call(
        functools.partial(kernel, pair_size, box_size, rank),
        out_shape=jax.ShapeDtypeStruct((box_size, chunks, points, shots), dtype),
        in_specs=[
            any_space,
            any_space,
            pl.BlockSpec(memory_space=pltpu.SMEM),
            pl.BlockSpec(memory_space=pltpu.VMEM),
            any_space,
        ],
        out_specs=any_space,
        scratch_shapes=[
            pltpu.VMEM((chunks, box_size, points, shots), dtype),
            pltpu.VMEM((chunks, box_size, points, rank), dtype),
            pltpu.VMEM((chunks, box_size, points, rank), dtype),
            pltpu.VMEM(block, dtype),
            pltpu.VMEM(block, dtype),
            pltpu.VMEM((box_levels, box_size, rank, shots), dtype),
            pltpu.VMEM((chunks, box_size, points, shots), dtype),
        ]
        + [pltpu.VMEM((chunks, box_size, 2 * rank, shots), dtype)] * pair_levels
        + [pltpu.SemaphoreType.DMA((chunks,))] * 4
        + [pltpu.SemaphoreType.DMA((pair_levels, chunks))] * 2
        + [pltpu.SemaphoreType.DMA((chunks, box_size))] * 2,
        compiler_params=pltpu.CompilerParams(
            collective_id=0, has_side_effects=True, vmem_limit_bytes=56 * 2**20
        ),
    )(
        sources.reshape(box_size, chunks, points, shots),
        basis_in.reshape(box_size, chunks, points, rank),
        kinds,
        couplings,
        basis_out.reshape(box_size, chunks, points, rank),
    )
    return wavefield.reshape(box_count, points, shots)


def solution(mesh):
    in_specs = (
        P(("pair", "box"), None, None),
        P(("pair", "box"), None),
        P(None, ("pair", "box")),
        P(),
        P(("pair", "box"), None),
    )
    out_specs = P(("pair", "box"), None, None)
    return jax.shard_map(body, mesh=mesh, in_specs=in_specs, out_specs=out_specs, check_vma=False)
```
